32 devices in a mesh: dp: 4 (over y, x), expert: 8 (over z, core).
Axes of the slice: x: 2, y: 2, z: 4, core: 2. Of those that a mesh axis runs over, the one named last changes fastest.
Arguments:
- tokens: bfloat16 [8192, 1024], P(('dp', 'expert')), may hold values from -6 to 6
- segment_ids: int32 [8192], P(('dp', 'expert')), may hold values from 0 to 12, as said below
- parent_ids: int32 [8192], P(('dp', 'expert')), may hold values from 0 to 10, as said below
- path_depth: int32 [8192], P(('dp', 'expert')), may hold values from 0 to 245, as said below
- routes: int32 [8192, 2], P(('dp', 'expert')), may hold values from 0 to 15, as said below
- slot_index: int32 [8192, 2], P(('dp', 'expert')), may hold values from 0 to 39, as said below
- gain_attn: bfloat16 [1024], P('dp'), may hold values from 0.5 to 1.5
- w_query: bfloat16 [1024, 1024], P('dp'), may hold values from -0.25 to 0.25
- w_key: bfloat16 [1024, 1024], P('dp'), may hold values from -0.25 to 0.25
- w_value: bfloat16 [1024, 1024], P('dp'), may hold values from -0.1875 to 0.1875
- w_out: bfloat16 [1024, 1024], P('dp'), may hold values from -0.75 to 0.75
- gain_moe: bfloat16 [1024], P('dp'), may hold values from 0.5 to 1.5
- w_router: bfloat16 [1024, 16], P('dp'), may hold values from -0.09375 to 0.09375
- w_gate: bfloat16 [16, 1024, 2816], P('expert', None, 'dp'), may hold values from -0.1875 to 0.1875
- w_up: bfloat16 [16, 1024, 2816], P('expert', None, 'dp'), may hold values from -0.1875 to 0.1875
- w_down: bfloat16 [16, 2816, 1024], P('expert', 'dp'), may hold values from -0.21875 to 0.21875
- cotangent: bfloat16 [8192, 1024], P(('dp', 'expert')), may hold values from -6 to 6
Outputs:
- output: bfloat16 [8192, 1024], P(('dp', 'expert'))
- token_grad: float32 [8192, 1024], P(('dp', 'expert'))
- gain_attn_grad: float32 [1024], P(('dp', 'expert'))
- query_grad: float32 [1024, 1024], P(('dp', 'expert'))
- key_grad: float32 [1024, 1024], P(('dp', 'expert'))
- value_grad: float32 [1024, 1024], P(('dp', 'expert'))
- out_proj_grad: float32 [1024, 1024], P(('dp', 'expert'))
- gain_moe_grad: float32 [1024], P(('dp', 'expert'))
- router_grad: float32 [1024, 16], P(('dp', 'expert'))
- gate_grad: float32 [16, 1024, 2816], P('expert', None, 'dp')
- up_grad: float32 [16, 1024, 2816], P('expert', None, 'dp')
- down_grad: float32 [16, 2816, 1024], P('expert', 'dp')
The draws below stay inside these ranges and needn't reach their ends.
Inputs may be any that keep to these rules, and one draw needn't show every extreme that they name: `segment_ids`: in each aligned block of 256 tokens (one tree sequence) segment ids never fall; 0 is the trunk, 1, 4, 7 and 10 are branches, each followed by its two leaves; every segment has one token or more. `parent_ids`: the id of the parent of the token's segment; 0 for the trunk and the branches. `path_depth`: trunk tokens count from 0, a branch continues after the trunk, a leaf after its branch; the bound is reached in some sequence. `routes`: a token's two experts differ; within the rows of one device each expert is named by at most 40 tokens, and one expert, the same on every device, by exactly 40. `slot_index`: within the rows of one device, pairs routed to the same expert have different slots.
All inputs are finite; a program needn't handle non-finite values.
Results may differ from the reference program's by a relative error of at most 0.015.
The reference program's roundings to bfloat16 on the way count: a program that leaves them out, or rounds other values in their place, can miss the bound.
Values may be sent and summed in bfloat16 or wider, within the bound.
A program may use at most 256 MiB of HBM per device.

```python
import jax
import jax.numpy as jnp
from jax import lax

HEADS = 16
HEAD_DIM = 64
D = 1024
FF = 2816
EXPERTS = 16
TOK_DEV = 256
CAP = 40
TOKENS = 8192


def tree_block(block_key, block_number):
    labels = jnp.arange(13)
    weights = jax.random.randint(block_key, (13,), 1, 9)
    weights = jnp.where((block_number == 0) & (labels > 2), 0, weights)
    spare_tokens = TOK_DEV - 13
    seg_lengths = 1 + weights * spare_tokens // jnp.sum(weights)
    seg_lengths = seg_lengths.at[0].add(TOK_DEV - jnp.sum(seg_lengths))
    seg_ends = jnp.cumsum(seg_lengths)
    seg_starts = seg_ends - seg_lengths
    within = labels % 3
    parents = jnp.where(labels == 0, 0, jnp.where(within == 1, 0, jnp.where(within == 2, labels - 1, labels - 2)))
    offsets = jnp.where(labels == 0, 0, jnp.where(within == 1, seg_lengths[0], seg_lengths[0] + seg_lengths[parents]))
    position = jnp.arange(TOK_DEV)
    segment = jnp.sum((position[:, None] >= seg_ends[None, :]).astype(jnp.int32), axis=1)
    depths = position - seg_starts[segment] + offsets[segment]
    return (segment.astype(jnp.int32), parents[segment].astype(jnp.int32), depths.astype(jnp.int32))


def tree_all(key):
    block_count = TOKENS // TOK_DEV
    block_keys = jax.random.split(jax.random.fold_in(key, 7), block_count)
    numbers = jnp.arange(block_count, dtype=jnp.int32)
    segment, parent, depths = jax.vmap(tree_block)(block_keys, numbers)
    return (segment.reshape(-1), parent.reshape(-1), depths.reshape(-1))


def routing_block(block_key, full_expert):
    mean_load = 2 * TOK_DEV // EXPERTS
    extra_load = CAP - mean_load
    key_order, key_spread, key_slot, key_token = jax.random.split(block_key, 4)
    ordering = jax.random.permutation(key_order, EXPERTS)
    shift_by = jnp.argmax(ordering == full_expert)
    ordering = jnp.roll(ordering, -shift_by)
    spreads = jax.random.randint(key_spread, (EXPERTS // 2,), 0, extra_load + 1)
    spreads = spreads.at[0].set(extra_load)
    paired = jnp.stack([mean_load + spreads, mean_load - spreads], axis=1).reshape(-1)
    expert_loads = jnp.zeros((EXPERTS,), jnp.int32).at[ordering].set(paired.astype(jnp.int32))
    cumulative = jnp.cumsum(expert_loads)
    pair_index = jnp.arange(2 * TOK_DEV)
    labels = jnp.sum((pair_index[:, None] >= cumulative[None, :]).astype(jnp.int32), axis=1)
    rank_in = pair_index - (cumulative - expert_loads)[labels]
    slot_orders = jax.vmap(lambda one_key: jax.random.permutation(one_key, CAP))(jax.random.split(key_slot, EXPERTS))
    placed = slot_orders[labels, rank_in]
    token_order = jax.random.permutation(key_token, TOK_DEV)
    route_pairs = jnp.stack([labels[:TOK_DEV], labels[TOK_DEV:]], axis=1).astype(jnp.int32)
    slot_pairs = jnp.stack([placed[:TOK_DEV], placed[TOK_DEV:]], axis=1).astype(jnp.int32)
    routes_out = jnp.zeros((TOK_DEV, 2), jnp.int32).at[token_order].set(route_pairs)
    slots_out = jnp.zeros((TOK_DEV, 2), jnp.int32).at[token_order].set(slot_pairs)
    return (routes_out, slots_out)


def routing_all(key):
    full_expert = jax.random.randint(jax.random.fold_in(key, 11), (), 0, EXPERTS)
    block_count = TOKENS // TOK_DEV
    block_keys = jax.random.split(jax.random.fold_in(key, 5), block_count)
    routes_all, slots_all = jax.vmap(lambda one_key: routing_block(one_key, full_expert))(block_keys)
    return (routes_all.reshape(-1, 2), slots_all.reshape(-1, 2))


def draw_segment_ids(key, part):
    return tree_all(key)[0]


def draw_parent_ids(key, part):
    return tree_all(key)[1]


def draw_path_depth(key, part):
    return tree_all(key)[2]


def draw_routes(key, part):
    return routing_all(key)[0]


def draw_slot_index(key, part):
    return routing_all(key)[1]


def spiked(entries, rng, source, target, blocks, factor):
    owner, partner = [(jnp.arange(entries.shape[dim]) // (entries.shape[dim] // blocks)).reshape([-1 if axis == dim else 1 for axis in range(entries.ndim)]) for dim in (source, target)]
    chosen = jax.random.permutation(rng, blocks)[partner]
    strong = (owner == chosen) | (owner == (partner + blocks // 2) % blocks)
    return jnp.where(strong, factor * entries, entries)


def levels(key, dims, cuts, low, top_value):
    def one(dim, parts):
        draws = jax.random.uniform(jax.random.fold_in(jax.random.fold_in(key, 6), dim), (parts,), jnp.float32, low / len(cuts), top_value / len(cuts))
        return jnp.repeat(jnp.exp(draws), dims[dim] // parts).reshape((-1,) + (1,) * (len(dims) - dim - 1))

    level = one(*cuts[0])
    for cut in cuts[1:]:
        level = level * one(*cut)
    return level


def bell_draw(rng, extent, spread, reach, cuts=(), held_as=jnp.bfloat16):
    gain = levels(rng, extent, cuts, -0.22, 0.18) if cuts else 1.0
    values = jax.random.normal(rng, extent, jnp.float32) * spread * gain
    return jnp.minimum(jnp.maximum(values, -reach), reach).astype(held_as)


def noise_with(key, shape, scale, most, cuts, heavy, held_as=jnp.bfloat16):
    drawn = scale * jax.random.normal(key, shape, jnp.float32)
    if cuts:
        drawn = drawn * levels(key, shape, cuts, -0.22, 0.18)
    return jnp.clip(spiked(drawn, jax.random.fold_in(key, 3), *heavy), -most, most).astype(held_as)


def setup_inputs(seed: int = 0) -> dict:
    keys = jax.random.split(jax.random.key(seed), 18)
    return {
        "tokens": noise_with(keys[0], (TOKENS, D), 1.0, 6.0, ((0, 32),), (0, 1, 32, 2.75)),
        "segment_ids": draw_segment_ids(jax.random.fold_in(keys[17], 71), 0),
        "parent_ids": draw_parent_ids(jax.random.fold_in(keys[17], 71), 0),
        "path_depth": draw_path_depth(jax.random.fold_in(keys[17], 71), 0),
        "routes": draw_routes(jax.random.fold_in(keys[17], 71), 0),
        "slot_index": draw_slot_index(jax.random.fold_in(keys[17], 71), 0),
        "gain_attn": jnp.clip(1.0 + 0.1 * jax.random.normal(keys[6], (D,), jnp.float32), 0.5, 1.5).astype(jnp.bfloat16),
        "w_query": bell_draw(keys[7], (D, D), (D // 2) ** -0.5, 0.25, ((0, 4),)),
        "w_key": bell_draw(keys[8], (D, D), (D // 2) ** -0.5, 0.25, ((0, 4),)),
        "w_value": bell_draw(keys[9], (D, D), D ** -0.5, 0.1875, ((0, 4),)),
        "w_out": bell_draw(keys[10], (D, D), (D // 16) ** -0.5, 0.75, ((0, 4),)),
        "gain_moe": jnp.clip(1.0 + 0.1 * jax.random.normal(keys[11], (D,), jnp.float32), 0.5, 1.5).astype(jnp.bfloat16),
        "w_router": bell_draw(keys[12], (D, EXPERTS), (4 * D) ** -0.5, 0.09375, ((0, 4),)),
        "w_gate": bell_draw(keys[13], (EXPERTS, D, FF), D ** -0.5, 0.1875, ((0, 8), (2, 4))),
        "w_up": bell_draw(keys[14], (EXPERTS, D, FF), D ** -0.5, 0.1875, ((0, 8), (2, 4))),
        "w_down": bell_draw(keys[15], (EXPERTS, FF, D), (FF // 4) ** -0.5, 0.21875, ((0, 8), (1, 4))),
        "cotangent": bell_draw(keys[16], (TOKENS, D), 1.0, 6.0, ((0, 32),)),
    }


EPS = 1e-06

@jax.custom_vjp
def low(v):
    return lax.optimization_barrier(v.astype(jnp.bfloat16)).astype(jnp.float32)

@jax.custom_vjp
def low_back(v):
    return v

def low_keep(v):
    return (low(v), None)

def low_pass(kept, grad):
    return (grad,)

def back_keep(v):
    return (v, None)

def back_low(kept, grad):
    return (low(grad),)
low.defvjp(low_keep, low_pass)
low_back.defvjp(back_keep, back_low)

def matmul(left, right):
    return jnp.dot(left, right, precision=lax.Precision.HIGHEST, preferred_element_type=jnp.float32)

def rms_scale(values, gain_vec):
    return values * lax.rsqrt(lax.optimization_barrier(jnp.mean(values * values, axis=-1, keepdims=True)) + EPS) * gain_vec

def rotate(values, cosine_part, sine_part):
    half_dim = values.shape[-1] // 2
    leading = values[..., :half_dim]
    trailing = values[..., half_dim:]
    return jnp.concatenate([leading * cosine_part - trailing * sine_part, leading * sine_part + trailing * cosine_part], axis=-1)

def angles(path_depth):
    half_dim = HEAD_DIM // 2
    frequency = 10000.0 ** (-jnp.arange(half_dim, dtype=jnp.float32) * 2.0 / HEAD_DIM)
    turned = path_depth.astype(jnp.float32)[:, None] * frequency[None, :]
    return (jnp.cos(turned)[:, None, :], jnp.sin(turned)[:, None, :])

def visible(segment, parent):
    position = jnp.arange(segment.shape[0])
    causal = position[None, :] <= position[:, None]
    related = (segment[None, :] == segment[:, None]) | (segment[None, :] == parent[:, None]) | (segment[None, :] == 0)
    return causal & related

def attend(pieces):
    queries, keys_in, values_in, segment, parent = pieces
    scores = low_back(jnp.einsum('qhd,khd->hqk', queries, keys_in, precision=lax.Precision.HIGHEST))
    scores = jnp.where(visible(segment, parent)[None], scores, -1e+30)
    row_top = lax.optimization_barrier(jnp.max(scores, axis=-1, keepdims=True))
    exponent = jnp.exp(scores - row_top)
    softmaxed = low(exponent / lax.optimization_barrier(jnp.sum(exponent, axis=-1, keepdims=True)))
    return jnp.einsum('hqk,khd->qhd', softmaxed, values_in, precision=lax.Precision.HIGHEST)

def expert_apply(pieces):
    rows_in, gate_w, up_w, down_w = pieces
    gate_pre = low_back(matmul(rows_in, gate_w))
    up_pre = low_back(matmul(rows_in, up_w))
    hidden = low(jax.nn.gelu(gate_pre, approximate=True) * up_pre)
    return low(low_back(matmul(hidden, down_w)))

def reference(tokens, segment_ids, parent_ids, path_depth, routes, slot_index, gain_attn, w_query, w_key, w_value, w_out, gain_moe, w_router, w_gate, w_up, w_down, cotangent):
    token_count = tokens.shape[0]
    seq_count = token_count // TOK_DEV
    cosine_part, sine_part = angles(path_depth)
    flat_slot = (jnp.arange(token_count, dtype=jnp.int32) // TOK_DEV)[:, None] * CAP + slot_index

    def shaped(array):
        return array.reshape((seq_count, TOK_DEV) + array.shape[1:])

    def forward(inputs, gain_one, query_w, key_w, value_w, out_w, gain_two, router_w, gate_w, up_w, down_w):
        normed = low(rms_scale(inputs, gain_one))
        queries = low_back(matmul(normed, query_w)).reshape(token_count, HEADS, HEAD_DIM)
        keys_all = low_back(matmul(normed, key_w)).reshape(token_count, HEADS, HEAD_DIM)
        values_all = low(low_back(matmul(normed, value_w))).reshape(token_count, HEADS, HEAD_DIM)
        queries = low(rotate(queries, cosine_part, sine_part) * 0.125)
        keys_all = low(rotate(keys_all, cosine_part, sine_part))
        attn_mixed = lax.map(jax.checkpoint(attend), (shaped(queries), shaped(keys_all), shaped(values_all), shaped(segment_ids), shaped(parent_ids)))
        attn_mixed = low(low_back(attn_mixed.reshape(token_count, D)))
        residual = inputs + low_back(matmul(attn_mixed, out_w))
        routed_in = low(rms_scale(residual, gain_two))
        logits = low_back(matmul(routed_in, router_w))
        chosen = jnp.take_along_axis(logits, routes, axis=1)
        gate_values = jax.nn.softmax(chosen, axis=1)
        buffers = jnp.zeros((EXPERTS, seq_count * CAP, D), jnp.float32)
        buffers = buffers.at[routes, flat_slot].set(jnp.broadcast_to(routed_in[:, None, :], (token_count, 2, D)))
        buffers = low_back(buffers)
        results = lax.map(jax.checkpoint(expert_apply), (buffers, gate_w, up_w, down_w))
        returned = results[routes, flat_slot]
        return residual + lax.optimization_barrier(jnp.sum(gate_values[:, :, None] * returned, axis=1))
    floats = (tokens.astype(jnp.float32), gain_attn.astype(jnp.float32), w_query.astype(jnp.float32), w_key.astype(jnp.float32), w_value.astype(jnp.float32), w_out.astype(jnp.float32), gain_moe.astype(jnp.float32), w_router.astype(jnp.float32), w_gate.astype(jnp.float32), w_up.astype(jnp.float32), w_down.astype(jnp.float32))
    result, pullback = jax.vjp(forward, *floats)
    gradients = pullback(cotangent.astype(jnp.float32))
    return (result.astype(jnp.bfloat16), gradients[0], gradients[1], gradients[2], gradients[3], gradients[4], gradients[5], gradients[6], gradients[7], gradients[8], gradients[9], gradients[10])
```

```python
import functools

import jax
import jax.numpy as jnp
from jax import lax
from jax.experimental import pallas as pl
from jax.experimental.pallas import tpu as pltpu
from jax.sharding import PartitionSpec as P

HEADS = 16
HEAD_DIM = 64
EXPERTS = 16
CAP = 40


EPS = 1e-06


def rms_scale(values, gain_vec):
    return values * lax.rsqrt(jnp.mean(values * values, axis=-1, keepdims=True) + EPS) * gain_vec


def rotate(values, cosine_part, sine_part):
    half_dim = values.shape[-1] // 2
    leading = values[..., :half_dim]
    trailing = values[..., half_dim:]
    return jnp.concatenate(
        [
            leading * cosine_part - trailing * sine_part,
            leading * sine_part + trailing * cosine_part,
        ],
        axis=-1,
    )


def angles(path_depth):
    half_dim = HEAD_DIM // 2
    frequency = 10000.0 ** (-jnp.arange(half_dim, dtype=jnp.float32) * 2.0 / HEAD_DIM)
    turned = path_depth.astype(jnp.float32)[:, None] * frequency[None, :]
    return (jnp.cos(turned)[:, None, :], jnp.sin(turned)[:, None, :])


def visible(segment, parent):
    position = jnp.arange(segment.shape[0])
    causal = position[None, :] <= position[:, None]
    related = (
        (segment[None, :] == segment[:, None])
        | (segment[None, :] == parent[:, None])
        | (segment[None, :] == 0)
    )
    return causal & related


def glu_apply(gate_part, up_part):
    return jax.nn.gelu(gate_part, approximate=True) * up_part


MESH_ID = pl.DeviceIdType.MESH
BF = jnp.bfloat16
F32 = jnp.float32


def places():
    d = lax.axis_index("dp")
    e = lax.axis_index("expert")
    px, py = d % 2, d // 2
    z, c = e // 2, e % 2
    xn = py * 2 + (1 - px)
    yn = (1 - py) * 2 + px
    dn = (1 - py) * 2 + (1 - px)
    return d, e, z, c, xn, yn, dn


def greet(peers):
    barrier = pltpu.get_barrier_semaphore()
    for peer in peers:
        pl.semaphore_signal(barrier, inc=1, device_id=peer, device_id_type=MESH_ID)
    pl.semaphore_wait(barrier, len(peers))


def push(src, dst, send, recv, peer):
    copy = pltpu.make_async_remote_copy(
        src_ref=src, dst_ref=dst, send_sem=send, recv_sem=recv, device_id=peer, device_id_type=MESH_ID
    )
    copy.start()
    return copy


def plus(*refs):
    total = refs[0][...].astype(F32)
    for ref in refs[1:]:
        total = total + ref[...].astype(F32)
    return total


def scatter_kernel(widths, *refs):
    n = len(widths)
    parts, outs = refs[:n], refs[n : 2 * n]
    scratch = refs[2 * n :]
    sib, acc, got, fin, zin = (scratch[i * n : (i + 1) * n] for i in range(5))
    send, recv = scratch[5 * n :]
    d, e, z, c, xn, yn, dn = places()
    sibling = (d, z * 2 + (1 - c))
    to_x, to_y = (xn, e), (yn, e)
    z_peers = [(d, ((z + k) % 4) * 2 + c) for k in (1, 2, 3)]
    greet([sibling, to_x, to_y] + z_peers)
    ops = []

    def go(u, slot, src, dst, peer):
        copy = push(src, dst, send.at[u, slot], recv.at[u, slot], peer)
        ops.append(copy)
        return copy

    first = [go(u, 0, parts[u].at[1 - c], sib[u], sibling) for u in range(n)]
    lo, hi = pl.ds(0, 2), pl.ds(2, 2)
    stage = []
    for u in range(n):
        first[u].wait_recv()
        acc[u][...] = plus(parts[u].at[c], sib[u]).astype(BF)
        a, g = acc[u], got[u]
        stage.append(
            (
                go(u, 1, a.at[dn, lo], g.at[0], to_x),
                go(u, 2, a.at[dn, hi], g.at[1], to_y),
                go(u, 3, a.at[xn, lo], g.at[2], to_x),
                go(u, 4, a.at[yn, hi], g.at[3], to_y),
            )
        )
    joined = []
    for u in range(n):
        a, g = acc[u], got[u]
        stage[u][0].wait_recv()
        a[yn, lo] = plus(a.at[yn, lo], g.at[0]).astype(BF)
        one = go(u, 5, a.at[yn, lo], g.at[4], to_y)
        stage[u][1].wait_recv()
        a[xn, hi] = plus(a.at[xn, hi], g.at[1]).astype(BF)
        two = go(u, 6, a.at[xn, hi], g.at[5], to_x)
        joined.append((one, two))
    last = []
    for u in range(n):
        a, g, f = acc[u], got[u], fin[u]
        stage[u][2].wait_recv()
        joined[u][0].wait_recv()
        f[lo] = plus(a.at[d, lo], g.at[2], g.at[4]).astype(BF)
        stage[u][3].wait_recv()
        joined[u][1].wait_recv()
        f[hi] = plus(a.at[d, hi], g.at[3], g.at[5]).astype(BF)
        last.append(
            [
                go(u, 7 + k, f.at[(z + k + 1) % 4], zin[u].at[k], z_peers[k])
                for k in range(3)
            ]
        )
    for u in range(n):
        for copy in last[u]:
            copy.wait_recv()
        outs[u][...] = plus(fin[u].at[z], zin[u].at[0], zin[u].at[1], zin[u].at[2])
    for copy in ops:
        copy.wait_send()


def scatter_rows(parts):
    widths = tuple(part.shape[-1] for part in parts)
    n = len(widths)
    space = pl.BlockSpec(memory_space=pltpu.VMEM)
    scratch = []
    for lead in ((4, 4), (4, 4), (6, 2), (4,), (3,)):
        scratch += [pltpu.VMEM(lead + (32, w), BF) for w in widths]
    return pl.pallas_call(
        functools.partial(scatter_kernel, widths),
        out_shape=[jax.ShapeDtypeStruct((32, w), F32) for w in widths],
        in_specs=[space] * n,
        out_specs=[space] * n,
        scratch_shapes=scratch + [pltpu.SemaphoreType.DMA((n, 10))] * 2,
        compiler_params=pltpu.CompilerParams(
            collective_id=1, has_side_effects=True, vmem_limit_bytes=40 << 20
        ),
    )(*parts)


def by_core(grad):
    return grad.astype(BF).reshape(4, 4, 2, 32, grad.shape[-1]).transpose(2, 0, 1, 3, 4)


def shards(
    tokens,
    segment_ids,
    parent_ids,
    path_depth,
    routes,
    slot_index,
    gain_attn,
    w_query,
    w_key,
    w_value,
    w_out,
    gain_moe,
    w_router,
    w_gate,
    w_up,
    w_down,
    cotangent,
):
    token_count = tokens.shape[0]
    model_width = tokens.shape[1]
    gain_one, query_w, key_w, value_w, out_w, gain_two, router_w = (
        lax.all_gather(gain_attn, "dp", axis=0, tiled=True),
        lax.all_gather(w_query, "dp", axis=0, tiled=True),
        lax.all_gather(w_key, "dp", axis=0, tiled=True),
        lax.all_gather(w_value, "dp", axis=0, tiled=True),
        lax.all_gather(w_out, "dp", axis=0, tiled=True),
        lax.all_gather(gain_moe, "dp", axis=0, tiled=True),
        lax.all_gather(w_router, "dp", axis=0, tiled=True),
    )
    gate_w, up_w, down_w = (w_gate, w_up, w_down)
    inputs = tokens.astype(jnp.float32)
    gain_onef = gain_one.astype(jnp.float32)
    gain_twof = gain_two.astype(jnp.float32)
    normed = rms_scale(inputs, gain_onef).astype(jnp.bfloat16)
    queries = jnp.dot(normed, query_w, preferred_element_type=jnp.float32).reshape(
        token_count, HEADS, HEAD_DIM
    )
    keys_all = jnp.dot(normed, key_w, preferred_element_type=jnp.float32).reshape(
        token_count, HEADS, HEAD_DIM
    )
    values_low = (
        jnp.dot(normed, value_w, preferred_element_type=jnp.float32)
        .astype(jnp.bfloat16)
        .reshape(token_count, HEADS, HEAD_DIM)
    )
    cosine_part, sine_part = angles(path_depth)
    queries_low = (rotate(queries, cosine_part, sine_part) * 0.125).astype(jnp.bfloat16)
    keys_low = rotate(keys_all, cosine_part, sine_part).astype(jnp.bfloat16)
    allowed = visible(segment_ids, parent_ids)[None]
    scores = jnp.einsum("qhd,khd->hqk", queries_low, keys_low, preferred_element_type=jnp.float32)
    scores = jnp.where(allowed, scores, -1e30)
    row_top = jnp.max(scores, axis=-1, keepdims=True)
    exponent = jnp.exp(scores - row_top)
    totals = jnp.sum(exponent, axis=-1, keepdims=True)
    log_total = row_top + jnp.log(totals)
    softmaxed = exponent / totals
    attn_mixed = jnp.einsum(
        "hqk,khd->qhd",
        softmaxed.astype(jnp.bfloat16),
        values_low,
        preferred_element_type=jnp.float32,
    )
    attn_mixed = attn_mixed.reshape(token_count, model_width).astype(jnp.bfloat16)
    residual = inputs + jnp.dot(attn_mixed, out_w, preferred_element_type=jnp.float32)
    routed_in = rms_scale(residual, gain_twof).astype(jnp.bfloat16)
    logits = jnp.dot(routed_in, router_w, preferred_element_type=jnp.float32)
    picker = (routes[:, :, None] == jnp.arange(EXPERTS)[None, None, :]).astype(jnp.float32)
    chosen = jnp.sum(picker * logits[:, None, :], axis=2)
    gate_values = jax.nn.softmax(chosen, axis=1)
    flat_slot = routes * CAP + slot_index
    owners = (
        jnp.zeros((EXPERTS * CAP,), jnp.int32)
        .at[flat_slot.reshape(-1)]
        .set(jnp.arange(2 * token_count, dtype=jnp.int32) + 1)
    )
    source_row = jnp.where(owners > 0, (owners - 1) // 2 + 1, 0)
    padded_in = jnp.concatenate([jnp.zeros((1, model_width), jnp.bfloat16), routed_in], axis=0)
    outgoing = padded_in[source_row].reshape(EXPERTS, CAP, model_width)
    arrived = lax.all_to_all(outgoing, "expert", split_axis=0, concat_axis=1, tiled=True)
    rows_used = lax.all_gather(arrived, "dp", axis=1, tiled=True)
    gate_pre = jnp.einsum("erd,edf->erf", rows_used, gate_w, preferred_element_type=jnp.float32)
    up_pre = jnp.einsum("erd,edf->erf", rows_used, up_w, preferred_element_type=jnp.float32)
    hidden = glu_apply(gate_pre, up_pre).astype(jnp.bfloat16)
    produced_terms = jnp.einsum("erf,efd->erd", hidden, down_w, preferred_element_type=jnp.float32)
    produced = lax.psum_scatter(
        produced_terms.astype(jnp.bfloat16), "dp", scatter_dimension=1, tiled=True
    )
    came_back = lax.all_to_all(produced, "expert", split_axis=1, concat_axis=0, tiled=True).reshape(
        EXPERTS * CAP, model_width
    )
    returned = came_back[flat_slot].astype(jnp.float32)
    moe_out = jnp.sum(gate_values[:, :, None] * returned, axis=1)
    output = (residual + moe_out).astype(jnp.bfloat16)
    upstream = cotangent.astype(jnp.float32)
    gate_value_grad = jnp.sum(upstream[:, None, :] * returned, axis=2)
    chosen_grad = gate_values * (
        gate_value_grad - jnp.sum(gate_values * gate_value_grad, axis=1, keepdims=True)
    )
    logit_grad = jnp.sum(picker * chosen_grad[:, :, None], axis=1).astype(jnp.bfloat16)
    pair_grad = (
        (gate_values[:, :, None] * upstream[:, None, :])
        .astype(jnp.bfloat16)
        .reshape(2 * token_count, model_width)
    )
    padded_grad = jnp.concatenate([jnp.zeros((1, model_width), jnp.bfloat16), pair_grad], axis=0)
    outgoing_grad = padded_grad[owners].reshape(EXPERTS, CAP, model_width)
    arrived_grad = lax.all_to_all(outgoing_grad, "expert", split_axis=0, concat_axis=1, tiled=True)
    grads_used = lax.all_gather(arrived_grad, "dp", axis=1, tiled=True)
    gate_back, up_back, down_back = (w_gate, w_up, w_down)
    hidden_grad = jnp.einsum(
        "erd,efd->erf", grads_used, down_back, preferred_element_type=jnp.float32
    )
    down_wgrad = jnp.einsum("erf,erd->efd", hidden, grads_used, preferred_element_type=jnp.float32)
    unused_value, glu_pull = jax.vjp(glu_apply, gate_pre, up_pre)
    gate_pre_grad, up_pre_grad = glu_pull(hidden_grad)
    gate_low = gate_pre_grad.astype(jnp.bfloat16)
    up_low = up_pre_grad.astype(jnp.bfloat16)
    gate_wgrad = jnp.einsum("erd,erf->edf", rows_used, gate_low, preferred_element_type=jnp.float32)
    up_wgrad = jnp.einsum("erd,erf->edf", rows_used, up_low, preferred_element_type=jnp.float32)
    rows_terms = jnp.einsum("erf,edf->erd", gate_low, gate_back, preferred_element_type=jnp.float32)
    rows_terms = rows_terms + jnp.einsum(
        "erf,edf->erd", up_low, up_back, preferred_element_type=jnp.float32
    )
    gate_sum, up_sum, down_sum = (gate_wgrad, up_wgrad, down_wgrad)
    rows_grad = lax.psum_scatter(
        rows_terms.astype(jnp.bfloat16), "dp", scatter_dimension=1, tiled=True
    )
    sent_back = lax.all_to_all(
        rows_grad, "expert", split_axis=1, concat_axis=0, tiled=True
    ).reshape(EXPERTS * CAP, model_width)
    query_back, key_back, value_back, out_back, router_back = (
        query_w,
        key_w,
        value_w,
        out_w,
        router_w,
    )
    routed_grad = jnp.sum(sent_back[flat_slot].astype(jnp.float32), axis=1)
    routed_grad = routed_grad + jnp.dot(
        logit_grad, router_back.T, preferred_element_type=jnp.float32
    )
    router_wgrad = jnp.einsum(
        "td,te->de", routed_in, logit_grad, preferred_element_type=jnp.float32
    )
    unused_norm, second_pull = jax.vjp(rms_scale, residual, gain_twof)
    residual_norm_grad, gain_two_grad = second_pull(routed_grad)
    residual_grad = upstream + residual_norm_grad
    branch_grad = residual_grad.astype(jnp.bfloat16)
    out_wgrad = jnp.einsum("td,te->de", attn_mixed, branch_grad, preferred_element_type=jnp.float32)
    mixed_grad = (
        jnp.dot(branch_grad, out_back.T, preferred_element_type=jnp.float32)
        .astype(jnp.bfloat16)
        .reshape(token_count, HEADS, HEAD_DIM)
    )
    scores = jnp.einsum("qhd,khd->hqk", queries_low, keys_low, preferred_element_type=jnp.float32)
    scores = jnp.where(allowed, scores, -1e30)
    softmaxed = jnp.exp(scores - log_total)
    value_low_grad = jnp.einsum(
        "hqk,qhd->khd",
        softmaxed.astype(jnp.bfloat16),
        mixed_grad,
        preferred_element_type=jnp.float32,
    )
    value_low_grad = value_low_grad.reshape(token_count, model_width).astype(jnp.bfloat16)
    weight_grad = jnp.einsum(
        "qhd,khd->hqk", mixed_grad, values_low, preferred_element_type=jnp.float32
    )
    score_grad = (
        softmaxed * (weight_grad - jnp.sum(softmaxed * weight_grad, axis=-1, keepdims=True))
    ).astype(jnp.bfloat16)
    query_rot_grad = (
        jnp.einsum("hqk,khd->qhd", score_grad, keys_low, preferred_element_type=jnp.float32) * 0.125
    )
    key_rot_grad = jnp.einsum(
        "hqk,qhd->khd", score_grad, queries_low, preferred_element_type=jnp.float32
    )
    query_low_grad = (
        rotate(query_rot_grad, cosine_part, -sine_part)
        .reshape(token_count, model_width)
        .astype(jnp.bfloat16)
    )
    key_low_grad = (
        rotate(key_rot_grad, cosine_part, -sine_part)
        .reshape(token_count, model_width)
        .astype(jnp.bfloat16)
    )
    query_wgrad = jnp.einsum(
        "td,te->de", normed, query_low_grad, preferred_element_type=jnp.float32
    )
    key_wgrad = jnp.einsum("td,te->de", normed, key_low_grad, preferred_element_type=jnp.float32)
    value_wgrad = jnp.einsum(
        "td,te->de", normed, value_low_grad, preferred_element_type=jnp.float32
    )
    normed_grad = jnp.dot(query_low_grad, query_back.T, preferred_element_type=jnp.float32)
    normed_grad = normed_grad + jnp.dot(
        key_low_grad, key_back.T, preferred_element_type=jnp.float32
    )
    normed_grad = normed_grad + jnp.dot(
        value_low_grad, value_back.T, preferred_element_type=jnp.float32
    )
    unused_first, first_pull = jax.vjp(rms_scale, inputs, gain_onef)
    input_norm_grad, gain_one_grad = first_pull(normed_grad)
    token_grad = residual_grad + input_norm_grad
    if lax.axis_size("dp") == 4 and lax.axis_size("expert") == 8:
        small = jnp.concatenate([router_wgrad, gain_one_grad[:, None], gain_two_grad[:, None]], axis=1)
        small = jnp.pad(small, ((0, 0), (0, 128 - small.shape[1])))
        got = scatter_rows([by_core(g) for g in (out_wgrad, value_wgrad, query_wgrad, key_wgrad, small)])
        return (
            output,
            token_grad,
            got[4][:, EXPERTS],
            got[2],
            got[3],
            got[1],
            got[0],
            got[4][:, EXPERTS + 1],
            got[4][:, :EXPERTS],
            gate_wgrad,
            up_wgrad,
            down_wgrad,
        )
    summed = (
        lax.psum_scatter(gain_one_grad, ("dp", "expert"), scatter_dimension=0, tiled=True),
        lax.psum_scatter(query_wgrad, ("dp", "expert"), scatter_dimension=0, tiled=True),
        lax.psum_scatter(key_wgrad, ("dp", "expert"), scatter_dimension=0, tiled=True),
        lax.psum_scatter(value_wgrad, ("dp", "expert"), scatter_dimension=0, tiled=True),
        lax.psum_scatter(out_wgrad, ("dp", "expert"), scatter_dimension=0, tiled=True),
        lax.psum_scatter(gain_two_grad, ("dp", "expert"), scatter_dimension=0, tiled=True),
        lax.psum_scatter(router_wgrad, ("dp", "expert"), scatter_dimension=0, tiled=True),
    )
    return (
        output,
        token_grad,
        summed[0],
        summed[1],
        summed[2],
        summed[3],
        summed[4],
        summed[5],
        summed[6],
        gate_sum,
        up_sum,
        down_sum,
    )


def solution(mesh):
    in_specs = (
        P(("dp", "expert"), None),
        P(("dp", "expert")),
        P(("dp", "expert")),
        P(("dp", "expert")),
        P(("dp", "expert"), None),
        P(("dp", "expert"), None),
        P("dp"),
        P("dp", None),
        P("dp", None),
        P("dp", None),
        P("dp", None),
        P("dp"),
        P("dp", None),
        P("expert", None, "dp"),
        P("expert", None, "dp"),
        P("expert", "dp", None),
        P(("dp", "expert"), None),
    )
    out_specs = (
        P(("dp", "expert"), None),
        P(("dp", "expert"), None),
        P(("dp", "expert")),
        P(("dp", "expert"), None),
        P(("dp", "expert"), None),
        P(("dp", "expert"), None),
        P(("dp", "expert"), None),
        P(("dp", "expert")),
        P(("dp", "expert"), None),
        P("expert", None, "dp"),
        P("expert", None, "dp"),
        P("expert", "dp", None),
    )
    return jax.shard_map(shards, mesh=mesh, in_specs=in_specs, out_specs=out_specs, check_vma=False)
```
